32 devices in a mesh: lon: 2 (over core), lat: 4 (over y, x), lead: 4 (over z).
Axes of the slice: x: 2, y: 2, z: 4, core: 2. Of those that a mesh axis runs over, the one named last changes fastest.
Arguments:
- activation: bfloat16 [16, 64, 4096], P('lead', 'lat', 'lon'), may hold values from -6 to 6
- pre_activation: bfloat16 [16, 64, 4096], P('lead', 'lat', 'lon'), may hold values from -8 to 8
- cotangent: bfloat16 [16, 64, 4096], P('lead', 'lat', 'lon'), may hold values from -6 to 6
- mode_weight: float32 [4608, 1024], P('lon'), may hold values from -1 to 1
- local_weight: float32 [32, 32], replicated, may hold values from -1 to 1
Outputs:
- input_grad: bfloat16 [16, 64, 4096], P('lead', 'lat', 'lon')
- mode_grad: float32 [4608, 1024], P('lon')
The draws below stay inside these ranges and needn't reach their ends.
All inputs are finite; a program needn't handle non-finite values.
Results may differ from the reference program's by a relative error of at most 0.001.
Values sent between devices are 32-bit elements; how exact they have to be, the bound alone decides.
A program may use at most 64 MiB of HBM per device.

```python
import math
import jax
import jax.numpy as jnp
from jax import lax

C = 32
MX = 24
MY = 24
MZ = 8
CX = 64
NX = 128
NY = 64
NZ = 16
MODES = 4608


def levels(own_key, shape, cuts, smallest, largest):
    def one(position, shards_of):
        draws = jax.random.uniform(jax.random.fold_in(jax.random.fold_in(own_key, 6), position), (shards_of,), jnp.float32, smallest / len(cuts), largest / len(cuts))
        return jnp.repeat(jnp.exp(draws), shape[position] // shards_of).reshape((-1,) + (1,) * (len(shape) - position - 1))

    level = one(*cuts[0])
    for cut in cuts[1:]:
        level = level * one(*cut)
    return level


def normal_values(own_key, dims, deviation, most, pieces=(), held_as=jnp.bfloat16):
    values = jax.random.normal(own_key, dims, jnp.float32) * deviation
    if len(pieces) > 0:
        values = levels(own_key, dims, pieces, -0.22, 0.18) * values
    return jnp.clip(values, min=-most, max=most).astype(held_as)


def setup_inputs(seed: int = 0) -> dict:
    splits = jax.random.split(jax.random.key(seed), 6)
    return {
        "activation": normal_values(splits[0], (NZ, NY, NX * C), 1.0, 6.0, ((0, 4), (1, 4), (2, 2))),
        "pre_activation": normal_values(splits[1], (NZ, NY, NX * C), 1.5, 8.0, ((0, 4), (1, 4), (2, 2))),
        "cotangent": normal_values(splits[2], (NZ, NY, NX * C), 1.0, 6.0, ((0, 4), (1, 4), (2, 2))),
        "mode_weight": normal_values(splits[3], (MODES, C * C), C ** -0.5, 1.0, ((0, 2),), jnp.float32),
        "local_weight": normal_values(splits[4], (C, C), C ** -0.5, 1.0, (), jnp.float32),
    }


def make_basis(length, modes, start, count, stride):
    half = modes // 2
    order = jnp.arange(modes, dtype=jnp.int32)
    freq = jnp.where(order < half, order, order - half + 1).astype(jnp.int32)
    cells = (start + stride * jnp.arange(count, dtype=jnp.int32)).astype(jnp.int32)
    turns = freq[:, None] * cells[None, :] % length
    angle = 2.0 * math.pi / length * turns.astype(jnp.float32)
    waves = jnp.where(order[:, None] < half, jnp.cos(angle), jnp.sin(angle))
    weights = jnp.where(order == 0, jnp.float32(math.sqrt(1.0 / length)), jnp.float32(math.sqrt(2.0 / length)))
    return waves * weights[:, None]

def gelu_slope(value):
    normal_cdf = 0.5 * (1.0 + jax.scipy.special.erf(value / math.sqrt(2.0)))
    density = jnp.exp(-0.5 * value * value) / math.sqrt(2.0 * math.pi)
    return normal_cdf + value * density

def forward_modes(field, lon_basis, lat_basis, lead_basis):
    highest = lax.Precision.HIGHEST
    step = jnp.einsum('zyxc,kx->zykc', field, lon_basis, precision=highest)
    step = jnp.einsum('zykc,ly->zklc', step, lat_basis, precision=highest)
    step = jnp.einsum('zklc,qz->klqc', step, lead_basis, precision=highest)
    return step.reshape(-1, step.shape[-1])

def back_cells(coeffs, lon_basis, lat_basis, lead_basis):
    highest = lax.Precision.HIGHEST
    blocks = coeffs.reshape(lon_basis.shape[0], lat_basis.shape[0], lead_basis.shape[0], coeffs.shape[-1])
    step = jnp.einsum('klqc,qz->zklc', blocks, lead_basis, precision=highest)
    step = jnp.einsum('zklc,ly->zykc', step, lat_basis, precision=highest)
    return jnp.einsum('zykc,kx->zyxc', step, lon_basis, precision=highest)

def to_cells(field):
    owners = NX // CX
    return field.reshape(NZ, NY, owners, CX, C).transpose(0, 1, 3, 2, 4).reshape(NZ, NY, NX, C)

def from_cells(field):
    owners = NX // CX
    return field.reshape(NZ, NY, CX, owners, C).transpose(0, 1, 3, 2, 4).reshape(NZ, NY, NX * C)

def reference(activation, pre_activation, cotangent, mode_weight, local_weight):
    lon_basis = make_basis(NX, MX, 0, NX, 1)
    lat_basis = make_basis(NY, MY, 0, NY, 1)
    lead_basis = make_basis(NZ, MZ, 0, NZ, 1)
    grad_pre = to_cells(cotangent.astype(jnp.float32)) * gelu_slope(to_cells(pre_activation.astype(jnp.float32)))
    coef = forward_modes(to_cells(activation.astype(jnp.float32)), lon_basis, lat_basis, lead_basis)
    gain = math.sqrt(NX * NY * NZ / MODES)
    spectral = gain * forward_modes(grad_pre, lon_basis, lat_basis, lead_basis)
    mode_grad = (coef[:, :, None] * spectral[:, None, :]).reshape(MODES, C * C)
    mixing = mode_weight.reshape(MODES, C, C)
    mode_adjoint = lax.optimization_barrier(jnp.sum(mixing * spectral[:, None, :], axis=2))
    spread = back_cells(mode_adjoint, lon_basis, lat_basis, lead_basis)
    local = jnp.einsum('zyxo,io->zyxi', grad_pre, local_weight, precision=lax.Precision.HIGHEST)
    input_grad = from_cells(spread + local)
    return (input_grad.astype(jnp.bfloat16), mode_grad)
```

```python
import functools
import math

import jax
import jax.numpy as jnp
import ml_dtypes
import numpy as np
from jax import lax
from jax.experimental import pallas as pl
from jax.experimental.pallas import tpu as pltpu
from jax.sharding import PartitionSpec as P

MX = 24
MY = 24
MZ = 8
MODES = 4608


def make_basis(length, modes, start, count, stride):
    half = modes // 2
    order = jnp.arange(modes, dtype=jnp.int32)
    freq = jnp.where(order < half, order, order - half + 1)
    cells = start + stride * jnp.arange(count, dtype=jnp.int32)
    turns = freq[:, None] * cells[None, :] % length
    angle = 2.0 * math.pi / length * turns.astype(jnp.float32)
    waves = jnp.where(order[:, None] < half, jnp.cos(angle), jnp.sin(angle))
    weights = jnp.where(
        order == 0, jnp.float32(math.sqrt(1.0 / length)), jnp.float32(math.sqrt(2.0 / length))
    )
    return waves * weights[:, None]


def gelu_slope(value):
    normal_cdf = 0.5 * (1.0 + jax.scipy.special.erf(value / math.sqrt(2.0)))
    density = jnp.exp(-0.5 * value * value) / math.sqrt(2.0 * math.pi)
    return normal_cdf + value * density


def back_cells(coeffs, lon_basis, lat_basis, lead_basis):
    highest = lax.Precision.HIGHEST
    blocks = coeffs.reshape(
        lon_basis.shape[0], lat_basis.shape[0], lead_basis.shape[0], coeffs.shape[-1]
    )
    step = jnp.einsum("klqc,qz->zklc", blocks, lead_basis, precision=highest)
    step = jnp.einsum("zklc,ly->zykc", step, lat_basis, precision=highest)
    return jnp.einsum("zykc,kx->zyxc", step, lon_basis, precision=highest)


def on_device(activation, pre_activation, cotangent, mode_weight, local_weight):
    highest = lax.Precision.HIGHEST
    channels = local_weight.shape[0]
    lead_cells, lat_cells, merged = activation.shape
    lon_cells = merged // channels
    lon_count = lax.axis_size("lon")
    lon_total = lon_cells * lon_count
    lat_total = lat_cells * lax.axis_size("lat")
    lead_total = lead_cells * lax.axis_size("lead")
    lon_basis = make_basis(lon_total, MX, lax.axis_index("lon"), lon_cells, lon_count)
    lat_basis = make_basis(lat_total, MY, lax.axis_index("lat") * lat_cells, lat_cells, 1)
    lead_basis = make_basis(lead_total, MZ, lax.axis_index("lead") * lead_cells, lead_cells, 1)
    shape4 = (lead_cells, lat_cells, lon_cells, channels)
    grad_pre = cotangent.astype(jnp.float32).reshape(shape4) * gelu_slope(
        pre_activation.astype(jnp.float32).reshape(shape4)
    )
    stacked = jnp.concatenate([activation.astype(jnp.float32).reshape(shape4), grad_pre], axis=3)
    doubled = 2 * channels
    along_lon = jnp.einsum("zyxc,kx->zykc", stacked, lon_basis, precision=highest)
    along_lat = jnp.einsum("zykc,ly->zklc", along_lon, lat_basis, precision=highest)
    partial_sum = jnp.einsum("zklc,qz->klqc", along_lat, lead_basis, precision=highest).reshape(
        -1, doubled
    )
    summed = lax.psum(partial_sum, ("lat", "lead"))
    owned = lax.psum_scatter(summed, "lon", scatter_dimension=0, tiled=True)
    gain = math.sqrt(lon_total * lat_total * lead_total / MODES)
    coef = owned[:, :channels]
    spectral = gain * owned[:, channels:]
    owned_count = owned.shape[0]
    mode_grad = (coef[:, :, None] * spectral[:, None, :]).reshape(owned_count, channels * channels)
    mixing = mode_weight.reshape(owned_count, channels, channels)
    owned_adjoint = jnp.sum(mixing * spectral[:, None, :], axis=2)
    every_mode = lax.all_gather(owned_adjoint, "lon", axis=0, tiled=True)
    spread = back_cells(every_mode, lon_basis, lat_basis, lead_basis)
    local = jnp.einsum("zyxo,io->zyxi", grad_pre, local_weight, precision=highest)
    input_grad = (spread + local).reshape(lead_cells, lat_cells, merged)
    return (input_grad.astype(jnp.bfloat16), mode_grad)


F32 = jnp.float32
BF16 = jnp.bfloat16


def host_basis(length, modes):
    half = modes // 2
    order = np.arange(modes)
    freq = np.where(order < half, order, order - half + 1)
    turns = (freq[:, None] * np.arange(length)[None, :]) % length
    angle = 2.0 * np.pi / length * turns
    waves = np.where(order[:, None] < half, np.cos(angle), np.sin(angle))
    weights = np.where(order == 0, np.sqrt(1.0 / length), np.sqrt(2.0 / length))
    return waves * weights[:, None]


def halves(table):
    table = np.asarray(table, np.float32)
    high = table.astype(ml_dtypes.bfloat16)
    low = (table - high.astype(np.float32)).astype(ml_dtypes.bfloat16)
    return np.stack([high, low])


def cut(value):
    high = value.astype(BF16)
    return high, (value - high.astype(F32)).astype(BF16)


NN = (((1,), (0,)), ((), ()))
NT = (((1,), (1,)), ((), ()))


def mm(a, b, dims=NN):
    return lax.dot_general(a, b, dims, preferred_element_type=F32)


def mm3(table, b, dims=NN):
    bh, bl = cut(b)
    return mm(table[0], bh, dims) + mm(table[0], bl, dims) + mm(table[1], bh, dims)


class Plan:
    def __init__(self, mesh, arg_shape, channels):
        self.nlon, self.nlat, self.nlead = (mesh.shape[n] for n in ("lon", "lat", "lead"))
        nz, ny, merged = arg_shape
        self.c = channels
        self.zl, self.yl = nz // self.nlead, ny // self.nlat
        self.nx = merged // channels
        self.xl = self.nx // self.nlon
        self.kp = MX // (self.nlon * self.nlat)
        self.kc = self.kp * channels
        self.lq = MY * MZ
        self.zy = self.zl * self.yl
        self.gain = math.sqrt(self.nx * ny * nz / MODES)
        eye_z, eye_l = np.eye(self.zl), np.eye(MY)
        bx, by, bz = host_basis(self.nx, MX), host_basis(ny, MY), host_basis(nz, MZ)
        c = channels
        lon_rows = np.stack(
            [np.repeat(bx[:, d :: self.nlon], c, axis=1) for d in range(self.nlon)]
        )
        self.lon_table = halves(lon_rows)
        self.same = np.tile(np.eye(c), (1, self.xl)).astype(ml_dtypes.bfloat16)
        by_p = by.reshape(MY, self.nlat, self.yl)
        bz_s = bz.reshape(MZ, self.nlead, self.zl)
        eye_fz = np.eye(2 * self.zl)
        self.lat_table = halves(
            np.stack([np.kron(eye_fz, by_p[:, p]) for p in range(self.nlat)])
        )
        lead = np.einsum("qsz,lm->slqzm", bz_s, eye_l)
        self.lead_table = halves(lead.reshape(self.nlead, self.lq, self.zl * MY))
        self.lead_back = halves(
            lead.transpose(0, 3, 4, 1, 2).reshape(self.nlead, self.zl * MY, self.lq)
        )
        back = np.einsum("lpy,zw->pzywl", by_p, eye_z)
        self.lat_back = halves(back.reshape(self.nlat * self.zy, self.zl * MY))
        cc = c * c
        self.tile = np.concatenate(
            [np.kron(np.eye(self.kp)[:, [k]], np.tile(np.eye(c), (1, 128 // c))) for k in range(self.kp)],
            axis=1,
        ).astype(ml_dtypes.bfloat16)
        self.spread = np.stack(
            [np.kron(np.eye(self.kp)[:, [k]], np.kron(np.eye(c), np.ones((1, c)))) for k in range(self.kp)]
        ).astype(ml_dtypes.bfloat16)
        self.gather = np.ascontiguousarray(self.spread.transpose(0, 2, 1))
        wide = 256 // c
        self.fan = np.tile(np.eye(c), (1, wide)).astype(np.float32)
        self.block = np.kron(np.eye(wide), np.ones((c, c))).astype(np.float32)
        self.cc = cc


def remote_kernel(
    plan, act, pre, cot, weight, lw, lon_t, same, lat_t, lead_t, lead_b, lat_b, tile, gather, fan, block,
    modes_out, h_out, loc_out,
    kx, xs, gbuf, sbuf, lonbuf, latsend, latrecv, leadbuf, wbuf, vbuf,
    wsem, lon_s, lon_r, lat_s, lat_r, lead_s, lead_r, g_s, g_r, v_s, v_r, f_s, f_r,
):
    pn = plan
    lon, lat, lead = (lax.axis_index(n) for n in ("lon", "lat", "lead"))
    mesh_id = pl.DeviceIdType.MESH
    other = 1 - lon
    wcopy = pltpu.make_async_copy(
        weight.at[pl.ds(pl.multiple_of(lat * (pn.kp * pn.lq), 8), pn.kp * pn.lq), :], wbuf, wsem
    )
    wcopy.start()
    barrier = pltpu.get_barrier_semaphore()
    pl.semaphore_signal(barrier, inc=1, device_id={"lon": other}, device_id_type=mesh_id)
    for d in range(1, pn.nlat):
        pl.semaphore_signal(
            barrier, inc=1, device_id={"lat": lax.rem(lat + d, pn.nlat)}, device_id_type=mesh_id
        )
    for d in range(1, pn.nlead):
        pl.semaphore_signal(
            barrier, inc=1, device_id={"lead": lax.rem(lead + d, pn.nlead)}, device_id_type=mesh_id
        )
    c = pn.c
    zy = pn.zy
    mask = same[...]
    for k in range(MX):
        for h in range(2):
            kx[h, k * c : (k + 1) * c, :] = lon_t[h, lon, k : k + 1, :] * mask

    v = pre[...].astype(F32)
    cdf = 0.5 * (1.0 + lax.erf(v * (1.0 / math.sqrt(2.0))))
    density = jnp.exp(-0.5 * v * v) * (1.0 / math.sqrt(2.0 * math.pi))
    grad = cot[...].astype(F32) * (cdf + v * density)
    gh, gl = cut(grad)
    xs[0:zy, :] = act[...]
    xs[zy : 2 * zy, :] = gh
    xs[2 * zy : 3 * zy, :] = jnp.zeros_like(gh)
    xs[3 * zy : 4 * zy, :] = gl
    half = MX // pn.nlon * c
    for turn in range(2):
        who = other if turn == 0 else lon
        rows = pl.ds(pl.multiple_of(who * half, half), half)
        p = mm(kx[0, rows, :], xs[...], NT)
        q = mm(kx[1, rows, :], xs[0 : 2 * zy, :], NT)
        sbuf[who] = p[:, 0 : 2 * zy] + p[:, 2 * zy :] + q
        if turn == 0:
            pl.semaphore_wait(barrier, 1 + (pn.nlat - 1) + (pn.nlead - 1))
            lon_copy = pltpu.make_async_remote_copy(
                src_ref=sbuf.at[other], dst_ref=lonbuf, send_sem=lon_s, recv_sem=lon_r,
                device_id={"lon": other}, device_id_type=mesh_id,
            )
            lon_copy.start()
    lon_copy.wait()
    lat_copies = []
    for d in list(range(1, pn.nlat)) + [0]:
        p = lax.rem(lat + d, pn.nlat)
        rows = pl.ds(pl.multiple_of(p * pn.kc, pn.kc), pn.kc)
        value = sbuf[lon, rows, :] + lonbuf[rows, :]
        if d == 0:
            latrecv[lat] = value
        else:
            latsend[d - 1] = value
            copy = pltpu.make_async_remote_copy(
                src_ref=latsend.at[d - 1], dst_ref=latrecv.at[lat],
                send_sem=lat_s.at[d - 1], recv_sem=lat_r.at[d - 1],
                device_id={"lat": p}, device_id_type=mesh_id,
            )
            copy.start()
            lat_copies.append(copy)
    highest = lax.Precision.HIGHEST
    left = lax.dot_general(fan[...], lw[...], (((0,), (1,)), ((), ())), precision=highest, preferred_element_type=F32)
    both = jnp.dot(left, fan[...], precision=highest, preferred_element_type=F32) * block[...]
    bh, bl = cut(both)
    for t in range(pn.xl * c // 256):
        cols = slice(t * 256, (t + 1) * 256)
        hi, lo = xs[zy : 2 * zy, cols], xs[3 * zy : 4 * zy, cols]
        loc_out[:, cols] = mm(hi, bh) + mm(lo, bh) + mm(hi, bl)
    for copy in lat_copies:
        copy.wait()
    total = None
    for p in range(pn.nlat):
        term = mm3((lat_t[0, p], lat_t[1, p]), latrecv[p], NT)
        total = term if total is None else total + term
    leadbuf[lead] = total
    lead_copies = []
    for d in range(1, pn.nlead):
        copy = pltpu.make_async_remote_copy(
            src_ref=leadbuf.at[lead], dst_ref=leadbuf.at[lead],
            send_sem=lead_s.at[d - 1], recv_sem=lead_r.at[d - 1],
            device_id={"lead": lax.rem(lead + d, pn.nlead)}, device_id_type=mesh_id,
        )
        copy.start()
        lead_copies.append(copy)
    for copy in lead_copies:
        copy.wait()
    zm = pn.zl * MY
    out = []
    for f in range(2):
        total = None
        for s in range(pn.nlead):
            term = mm3((lead_t[0, s], lead_t[1, s]), leadbuf[s, f * zm : (f + 1) * zm, :])
            total = term if total is None else total + term
        out.append(total)
    coef, spectral = out[0], out[1] * pn.gain
    modes_out[lat, 0] = coef
    modes_out[lat, 1] = spectral
    g_copies = []
    for d in range(1, pn.nlat):
        copy = pltpu.make_async_remote_copy(
            src_ref=modes_out.at[lat], dst_ref=modes_out.at[lat],
            send_sem=g_s.at[d - 1], recv_sem=g_r.at[d - 1],
            device_id={"lat": lax.rem(lat + d, pn.nlat)}, device_id_type=mesh_id,
        )
        g_copies.append(copy)
    wcopy.wait()
    sh, sl = cut(spectral)
    wide = mm(sh, tile[...]) + mm(sl, tile[...])
    adjoint = None
    for k in range(pn.kp):
        four = wide[:, k * 128 : (k + 1) * 128]
        prod = wbuf[k * pn.lq : (k + 1) * pn.lq, :] * jnp.concatenate([four] * (pn.cc // 128), axis=1)
        ph, plow = cut(prod)
        term = mm(ph, gather[k]) + mm(plow, gather[k])
        adjoint = term if adjoint is None else adjoint + term
    mine = mm3((lead_b[0, lead], lead_b[1, lead]), adjoint)
    cells = mm3((lat_b[0], lat_b[1]), mine)
    for p in range(pn.nlat):
        vbuf[p] = cells[p * zy : (p + 1) * zy, :]
    h_out[lon, lat] = vbuf[lat]
    v_copies = []
    for d in range(1, pn.nlat):
        p = lax.rem(lat + d, pn.nlat)
        copy = pltpu.make_async_remote_copy(
            src_ref=vbuf.at[p], dst_ref=h_out.at[lon, lat],
            send_sem=v_s.at[d - 1], recv_sem=v_r.at[d - 1],
            device_id={"lat": p}, device_id_type=mesh_id,
        )
        copy.start()
        v_copies.append(copy)
    for copy in g_copies:
        copy.start()
    f_copies = []
    for d in range(pn.nlat):
        if d > 0:
            v_copies[d - 1].wait_recv()
        s = lax.rem(lat + pn.nlat - d, pn.nlat)
        copy = pltpu.make_async_remote_copy(
            src_ref=h_out.at[lon, s], dst_ref=h_out.at[lon, s],
            send_sem=f_s.at[d], recv_sem=f_r.at[d],
            device_id={"lon": other}, device_id_type=mesh_id,
        )
        copy.start()
        f_copies.append(copy)
    for copy in v_copies:
        copy.wait_send()
    for copy in f_copies:
        copy.wait()
    for copy in g_copies:
        copy.wait()


def finish_kernel(plan, modes, h_in, loc, lon_t, same, tile, spread, grad_out, mode_grad):
    pn = plan
    step = pl.program_id(0)
    lon = lax.axis_index("lon")
    c = pn.c
    coef, spectral = modes[0, 0], modes[0, 1]
    ch, cl = cut(coef)
    sh, sl = cut(spectral)
    r, t = spread[0], tile[...]
    s4 = mm(sh, t) + mm(sl, t)
    for j in range(pn.cc // 256):
        cols = slice(j * 256, (j + 1) * 256)
        big = mm(ch, r[:, cols]) + mm(cl, r[:, cols])
        mode_grad[:, cols] = big * jnp.concatenate([s4, s4], axis=1)

    @pl.when(step < pn.xl * c // 256)
    def _():
        cols = pl.ds(pl.multiple_of(step * 256, 256), 256)
        mask = same[:, 0:256]
        total = loc[:, cols]
        for g in range(pn.nlon * pn.nlat):
            parts = []
            for h in range(2):
                rows = [lon_t[h, lon, k : k + 1, cols] * mask for k in range(g * pn.kp, (g + 1) * pn.kp)]
                parts.append(jnp.concatenate(rows, axis=0))
            hh, hl = cut(h_in[g // pn.nlat, g % pn.nlat])
            total += mm(hh, parts[0]) + mm(hl, parts[0]) + mm(hh, parts[1])
        grad_out[:, cols] = total.astype(BF16)


def fast_device(plan, activation, pre_activation, cotangent, mode_weight, local_weight):
    pn = plan
    merged = activation.shape[2]
    flat = [v.reshape(pn.zy, merged) for v in (activation, pre_activation, cotangent)]
    vm = pl.BlockSpec(memory_space=pltpu.VMEM)
    hbm = pl.BlockSpec(memory_space=pl.ANY)
    half = MX // pn.nlon * pn.c
    dma = pltpu.SemaphoreType.DMA
    modes, h, loc = pl.pallas_call(
        functools.partial(remote_kernel, pn),
        out_shape=(
            jax.ShapeDtypeStruct((pn.nlat, 2, pn.lq, pn.kc), F32),
            jax.ShapeDtypeStruct((pn.nlon, pn.nlat, pn.zy, pn.kc), F32),
            jax.ShapeDtypeStruct((pn.zy, merged), F32),
        ),
        in_specs=[vm] * 3 + [hbm] + [vm] * 11,
        out_specs=(vm,) * 3,
        scratch_shapes=[
            pltpu.VMEM((2, MX * pn.c, merged), BF16),
            pltpu.VMEM((4 * pn.zy, merged), BF16),
            pltpu.VMEM((8, 128), F32),
            pltpu.VMEM((pn.nlon, half, 2 * pn.zy), F32),
            pltpu.VMEM((half, 2 * pn.zy), F32),
            pltpu.VMEM((pn.nlat - 1, pn.kc, 2 * pn.zy), F32),
            pltpu.VMEM((pn.nlat, pn.kc, 2 * pn.zy), F32),
            pltpu.VMEM((pn.nlead, 2 * pn.zl * MY, pn.kc), F32),
            pltpu.VMEM((pn.kp * pn.lq, pn.cc), F32),
            pltpu.VMEM((pn.nlat, pn.zy, pn.kc), F32),
            dma, dma, dma,
            dma((pn.nlat - 1,)), dma((pn.nlat - 1,)),
            dma((pn.nlead - 1,)), dma((pn.nlead - 1,)),
            dma((pn.nlat - 1,)), dma((pn.nlat - 1,)),
            dma((pn.nlat - 1,)), dma((pn.nlat - 1,)),
            dma((pn.nlat,)), dma((pn.nlat,)),
        ],
        compiler_params=pltpu.CompilerParams(
            collective_id=0, has_side_effects=True, vmem_limit_bytes=56 * 2**20
        ),
        name="modes",
    )(
        *flat, mode_weight, local_weight, pn.lon_table, pn.same, pn.lat_table, pn.lead_table,
        pn.lead_back, pn.lat_back, pn.tile, pn.gather, pn.fan, pn.block,
    )
    whole = lambda shape: pl.BlockSpec(shape, lambda i: (0,) * len(shape))
    grad, mode_grad = pl.pallas_call(
        functools.partial(finish_kernel, pn),
        grid=(pn.nlat * pn.kp,),
        out_shape=(
            jax.ShapeDtypeStruct((pn.zy, merged), BF16),
            jax.ShapeDtypeStruct((pn.nlat * pn.kp * pn.lq, pn.cc), F32),
        ),
        in_specs=[
            pl.BlockSpec((1, 2, pn.lq, pn.kc), lambda i: (i // pn.kp, 0, 0, 0)),
            whole(h.shape), whole(loc.shape), whole(pn.lon_table.shape), whole(pn.same.shape),
            pl.BlockSpec((pn.kc, 128), lambda i: (0, i % pn.kp)),
            pl.BlockSpec((1, pn.kc, pn.cc), lambda i: (i % pn.kp, 0, 0)),
        ],
        out_specs=(whole((pn.zy, merged)), pl.BlockSpec((pn.lq, pn.cc), lambda i: (i, 0))),
        compiler_params=pltpu.CompilerParams(vmem_limit_bytes=40 * 2**20),
        name="finish",
    )(modes, h, loc, pn.lon_table, pn.same, pn.tile, pn.spread)
    return grad.reshape(activation.shape), mode_grad


def solution(mesh):
    in_specs = (
        P("lead", "lat", "lon"),
        P("lead", "lat", "lon"),
        P("lead", "lat", "lon"),
        P("lon", None),
        P(),
    )
    out_specs = (P("lead", "lat", "lon"), P("lon", None))

    def whole(*args):
        shape = args[0].shape
        channels = args[4].shape[0]
        body = on_device
        if (
            mesh.shape["lon"] == 2
            and MX % (mesh.shape["lon"] * mesh.shape["lat"]) == 0
            and MX * MY * MZ == args[3].shape[0]
            and shape[2] // mesh.shape["lon"] % 256 == 0
            and 128 % channels == 0
        ):
            body = functools.partial(fast_device, Plan(mesh, shape, channels))
        return jax.shard_map(
            body, mesh=mesh, in_specs=in_specs, out_specs=out_specs, check_vma=False
        )(*args)

    return whole
```

```python
import functools
import math

import jax
import jax.numpy as jnp
import ml_dtypes
import numpy as np
from jax import lax
from jax.experimental import pallas as pl
from jax.experimental.pallas import tpu as pltpu
from jax.sharding import PartitionSpec as P

MX = 24
MY = 24
MZ = 8
MODES = 4608


def make_basis(length, modes, start, count, stride):
    half = modes // 2
    order = jnp.arange(modes, dtype=jnp.int32)
    freq = jnp.where(order < half, order, order - half + 1)
    cells = start + stride * jnp.arange(count, dtype=jnp.int32)
    turns = freq[:, None] * cells[None, :] % length
    angle = 2.0 * math.pi / length * turns.astype(jnp.float32)
    waves = jnp.where(order[:, None] < half, jnp.cos(angle), jnp.sin(angle))
    weights = jnp.where(
        order == 0, jnp.float32(math.sqrt(1.0 / length)), jnp.float32(math.sqrt(2.0 / length))
    )
    return waves * weights[:, None]


def gelu_slope(value):
    normal_cdf = 0.5 * (1.0 + jax.scipy.special.erf(value / math.sqrt(2.0)))
    density = jnp.exp(-0.5 * value * value) / math.sqrt(2.0 * math.pi)
    return normal_cdf + value * density


def back_cells(coeffs, lon_basis, lat_basis, lead_basis):
    highest = lax.Precision.HIGHEST
    blocks = coeffs.reshape(
        lon_basis.shape[0], lat_basis.shape[0], lead_basis.shape[0], coeffs.shape[-1]
    )
    step = jnp.einsum("klqc,qz->zklc", blocks, lead_basis, precision=highest)
    step = jnp.einsum("zklc,ly->zykc", step, lat_basis, precision=highest)
    return jnp.einsum("zykc,kx->zyxc", step, lon_basis, precision=highest)


def on_device(activation, pre_activation, cotangent, mode_weight, local_weight):
    highest = lax.Precision.HIGHEST
    channels = local_weight.shape[0]
    lead_cells, lat_cells, merged = activation.shape
    lon_cells = merged // channels
    lon_count = lax.axis_size("lon")
    lon_total = lon_cells * lon_count
    lat_total = lat_cells * lax.axis_size("lat")
    lead_total = lead_cells * lax.axis_size("lead")
    lon_basis = make_basis(lon_total, MX, lax.axis_index("lon"), lon_cells, lon_count)
    lat_basis = make_basis(lat_total, MY, lax.axis_index("lat") * lat_cells, lat_cells, 1)
    lead_basis = make_basis(lead_total, MZ, lax.axis_index("lead") * lead_cells, lead_cells, 1)
    shape4 = (lead_cells, lat_cells, lon_cells, channels)
    grad_pre = cotangent.astype(jnp.float32).reshape(shape4) * gelu_slope(
        pre_activation.astype(jnp.float32).reshape(shape4)
    )
    stacked = jnp.concatenate([activation.astype(jnp.float32).reshape(shape4), grad_pre], axis=3)
    doubled = 2 * channels
    along_lon = jnp.einsum("zyxc,kx->zykc", stacked, lon_basis, precision=highest)
    along_lat = jnp.einsum("zykc,ly->zklc", along_lon, lat_basis, precision=highest)
    partial_sum = jnp.einsum("zklc,qz->klqc", along_lat, lead_basis, precision=highest).reshape(
        -1, doubled
    )
    summed = lax.psum(partial_sum, ("lat", "lead"))
    owned = lax.psum_scatter(summed, "lon", scatter_dimension=0, tiled=True)
    gain = math.sqrt(lon_total * lat_total * lead_total / MODES)
    coef = owned[:, :channels]
    spectral = gain * owned[:, channels:]
    owned_count = owned.shape[0]
    mode_grad = (coef[:, :, None] * spectral[:, None, :]).reshape(owned_count, channels * channels)
    mixing = mode_weight.reshape(owned_count, channels, channels)
    owned_adjoint = jnp.sum(mixing * spectral[:, None, :], axis=2)
    every_mode = lax.all_gather(owned_adjoint, "lon", axis=0, tiled=True)
    spread = back_cells(every_mode, lon_basis, lat_basis, lead_basis)
    local = jnp.einsum("zyxo,io->zyxi", grad_pre, local_weight, precision=highest)
    input_grad = (spread + local).reshape(lead_cells, lat_cells, merged)
    return (input_grad.astype(jnp.bfloat16), mode_grad)


F32 = jnp.float32
BF16 = jnp.bfloat16


def host_basis(length, modes):
    half = modes // 2
    order = np.arange(modes)
    freq = np.where(order < half, order, order - half + 1)
    turns = (freq[:, None] * np.arange(length)[None, :]) % length
    angle = 2.0 * np.pi / length * turns
    waves = np.where(order[:, None] < half, np.cos(angle), np.sin(angle))
    weights = np.where(order == 0, np.sqrt(1.0 / length), np.sqrt(2.0 / length))
    return waves * weights[:, None]


def halves(table):
    table = np.asarray(table, np.float32)
    high = table.astype(ml_dtypes.bfloat16)
    low = (table - high.astype(np.float32)).astype(ml_dtypes.bfloat16)
    return np.stack([high, low])


def cut(value):
    high = value.astype(BF16)
    return high, (value - high.astype(F32)).astype(BF16)


NN = (((1,), (0,)), ((), ()))
NT = (((1,), (1,)), ((), ()))


def mm(a, b, dims=NN):
    return lax.dot_general(a, b, dims, preferred_element_type=F32)


def mm3(table, b, dims=NN):
    bh, bl = cut(b)
    return mm(table[0], bh, dims) + mm(table[0], bl, dims) + mm(table[1], bh, dims)


class Plan:
    def __init__(self, mesh, arg_shape, channels):
        self.nlon, self.nlat, self.nlead = (mesh.shape[n] for n in ("lon", "lat", "lead"))
        nz, ny, merged = arg_shape
        self.c = channels
        self.zl, self.yl = nz // self.nlead, ny // self.nlat
        self.nx = merged // channels
        self.xl = self.nx // self.nlon
        self.kp = MX // (self.nlon * self.nlat)
        self.kc = self.kp * channels
        self.lq = MY * MZ
        self.zy = self.zl * self.yl
        self.gain = math.sqrt(self.nx * ny * nz / MODES)
        eye_z, eye_l = np.eye(self.zl), np.eye(MY)
        bx, by, bz = host_basis(self.nx, MX), host_basis(ny, MY), host_basis(nz, MZ)
        c = channels
        lon_rows = np.stack(
            [np.repeat(bx[:, d :: self.nlon], c, axis=1) for d in range(self.nlon)]
        )
        self.lon_table = halves(lon_rows)
        self.same = np.tile(np.eye(c), (1, self.xl)).astype(ml_dtypes.bfloat16)
        by_p = by.reshape(MY, self.nlat, self.yl)
        bz_s = bz.reshape(MZ, self.nlead, self.zl)
        eye_fz = np.eye(2 * self.zl)
        self.lat_table = halves(
            np.stack([np.kron(eye_fz, by_p[:, p]) for p in range(self.nlat)])
        )
        lead = np.einsum("qsz,lm->slqzm", bz_s, eye_l)
        self.lead_table = halves(lead.reshape(self.nlead, self.lq, self.zl * MY))
        self.lead_back = halves(
            lead.transpose(0, 3, 4, 1, 2).reshape(self.nlead, self.zl * MY, self.lq)
        )
        back = np.einsum("lpy,zw->pzywl", by_p, eye_z)
        self.lat_back = halves(back.reshape(self.nlat * self.zy, self.zl * MY))
        cc = c * c
        self.tile = np.concatenate(
            [np.kron(np.eye(self.kp)[:, [k]], np.tile(np.eye(c), (1, 128 // c))) for k in range(self.kp)],
            axis=1,
        ).astype(ml_dtypes.bfloat16)
        self.spread = np.stack(
            [np.kron(np.eye(self.kp)[:, [k]], np.kron(np.eye(c), np.ones((1, c)))) for k in range(self.kp)]
        ).astype(ml_dtypes.bfloat16)
        self.gather = np.ascontiguousarray(self.spread.transpose(0, 2, 1))
        wide = 256 // c
        self.fan = np.tile(np.eye(c), (1, wide)).astype(np.float32)
        self.block = np.kron(np.eye(wide), np.ones((c, c))).astype(np.float32)
        self.cc = cc


def remote_kernel(
    plan, act, pre, cot, weight, lw, lon_t, same, lat_t, lead_t, lead_b, lat_b, tile, gather, fan, block,
    modes_out, h_out, loc_out,
    kx, xs, sbuf, lonbuf, latsend, latrecv, leadbuf, wbuf, vbuf,
    wsem, lon_s, lon_r, lat_s, lat_r, lead_s, lead_r, g_s, g_r, v_s, v_r, f_s, f_r,
):
    pn = plan
    lon, lat, lead = (lax.axis_index(n) for n in ("lon", "lat", "lead"))
    mesh_id = pl.DeviceIdType.MESH
    other = 1 - lon
    wcopy = pltpu.make_async_copy(
        weight.at[pl.ds(pl.multiple_of(lat * (pn.kp * pn.lq), 8), pn.kp * pn.lq), :], wbuf, wsem
    )
    wcopy.start()
    barrier = pltpu.get_barrier_semaphore()
    pl.semaphore_signal(barrier, inc=1, device_id={"lon": other}, device_id_type=mesh_id)
    for d in range(1, pn.nlat):
        pl.semaphore_signal(
            barrier, inc=1, device_id={"lat": lax.rem(lat + d, pn.nlat)}, device_id_type=mesh_id
        )
    for d in range(1, pn.nlead):
        pl.semaphore_signal(
            barrier, inc=1, device_id={"lead": lax.rem(lead + d, pn.nlead)}, device_id_type=mesh_id
        )
    c = pn.c
    zy = pn.zy
    mask = same[...]
    for k in range(MX):
        for h in range(2):
            kx[h, k * c : (k + 1) * c, :] = lon_t[h, lon, k : k + 1, :] * mask

    v = pre[...].astype(F32)
    cdf = 0.5 * (1.0 + lax.erf(v * (1.0 / math.sqrt(2.0))))
    density = jnp.exp(-0.5 * v * v) * (1.0 / math.sqrt(2.0 * math.pi))
    grad = cot[...].astype(F32) * (cdf + v * density)
    gh, gl = cut(grad)
    xs[0:zy, :] = act[...]
    xs[zy : 2 * zy, :] = gh
    xs[2 * zy : 3 * zy, :] = jnp.zeros_like(gh)
    xs[3 * zy : 4 * zy, :] = gl
    half = MX // pn.nlon * c
    for turn in range(2):
        who = other if turn == 0 else lon
        rows = pl.ds(pl.multiple_of(who * half, half), half)
        p = mm(kx[0, rows, :], xs[...], NT)
        q = mm(kx[1, rows, :], xs[0 : 2 * zy, :], NT)
        sbuf[who] = p[:, 0 : 2 * zy] + p[:, 2 * zy :] + q
        if turn == 0:
            pl.semaphore_wait(barrier, 1 + (pn.nlat - 1) + (pn.nlead - 1))
            lon_copy = pltpu.make_async_remote_copy(
                src_ref=sbuf.at[other], dst_ref=lonbuf, send_sem=lon_s, recv_sem=lon_r,
                device_id={"lon": other}, device_id_type=mesh_id,
            )
            lon_copy.start()
    lon_copy.wait()
    lat_copies = []
    for d in list(range(1, pn.nlat)) + [0]:
        p = lax.rem(lat + d, pn.nlat)
        rows = pl.ds(pl.multiple_of(p * pn.kc, pn.kc), pn.kc)
        value = sbuf[lon, rows, :] + lonbuf[rows, :]
        if d == 0:
            latrecv[lat] = value
        else:
            latsend[d - 1] = value
            copy = pltpu.make_async_remote_copy(
                src_ref=latsend.at[d - 1], dst_ref=latrecv.at[lat],
                send_sem=lat_s.at[d - 1], recv_sem=lat_r.at[d - 1],
                device_id={"lat": p}, device_id_type=mesh_id,
            )
            copy.start()
            lat_copies.append(copy)
    highest = lax.Precision.HIGHEST
    left = lax.dot_general(fan[...], lw[...], (((0,), (1,)), ((), ())), precision=highest, preferred_element_type=F32)
    both = jnp.dot(left, fan[...], precision=highest, preferred_element_type=F32) * block[...]
    bh, bl = cut(both)
    for t in range(pn.xl * c // 256):
        cols = slice(t * 256, (t + 1) * 256)
        hi, lo = xs[zy : 2 * zy, cols], xs[3 * zy : 4 * zy, cols]
        loc_out[:, cols] = mm(hi, bh) + mm(lo, bh) + mm(hi, bl)
    for copy in lat_copies:
        copy.wait()
    total = None
    for p in range(pn.nlat):
        term = mm3((lat_t[0, p], lat_t[1, p]), latrecv[p], NT)
        total = term if total is None else total + term
    zm = pn.zl * MY
    lead_copies = {}
    for f in (1, 0):
        leadbuf[lead, f] = total[f * zm : (f + 1) * zm, :]
        for d in range(1, pn.nlead):
            copy = pltpu.make_async_remote_copy(
                src_ref=leadbuf.at[lead, f], dst_ref=leadbuf.at[lead, f],
                send_sem=lead_s.at[f, d - 1], recv_sem=lead_r.at[f, d - 1],
                device_id={"lead": lax.rem(lead + d, pn.nlead)}, device_id_type=mesh_id,
            )
            copy.start()
            lead_copies[f, d] = copy
    g_copies = []

    def finish_lead(f):
        for d in range(1, pn.nlead):
            lead_copies[f, d].wait()
        total = None
        for s in range(pn.nlead):
            term = mm3((lead_t[0, s], lead_t[1, s]), leadbuf[s, f])
            total = term if total is None else total + term
        if f == 1:
            total = total * pn.gain
        modes_out[lat, f] = total
        for d in range(1, pn.nlat):
            copy = pltpu.make_async_remote_copy(
                src_ref=modes_out.at[lat, f], dst_ref=modes_out.at[lat, f],
                send_sem=g_s.at[f, d - 1], recv_sem=g_r.at[f, d - 1],
                device_id={"lat": lax.rem(lat + d, pn.nlat)}, device_id_type=mesh_id,
            )
            copy.start()
            g_copies.append(copy)
        return total

    spectral = finish_lead(1)
    wcopy.wait()
    sh, sl = cut(spectral)
    wide = mm(sh, tile[...]) + mm(sl, tile[...])
    adjoint = None
    for k in range(pn.kp):
        four = wide[:, k * 128 : (k + 1) * 128]
        prod = wbuf[k * pn.lq : (k + 1) * pn.lq, :] * jnp.concatenate([four] * (pn.cc // 128), axis=1)
        ph, plow = cut(prod)
        term = mm(ph, gather[k]) + mm(plow, gather[k])
        adjoint = term if adjoint is None else adjoint + term
    mine = mm3((lead_b[0, lead], lead_b[1, lead]), adjoint)
    cells = mm3((lat_b[0], lat_b[1]), mine)
    for p in range(pn.nlat):
        vbuf[p] = cells[p * zy : (p + 1) * zy, :]
    h_out[lon, lat] = vbuf[lat]
    v_copies = []
    for d in range(1, pn.nlat):
        p = lax.rem(lat + d, pn.nlat)
        copy = pltpu.make_async_remote_copy(
            src_ref=vbuf.at[p], dst_ref=h_out.at[lon, lat],
            send_sem=v_s.at[d - 1], recv_sem=v_r.at[d - 1],
            device_id={"lat": p}, device_id_type=mesh_id,
        )
        copy.start()
        v_copies.append(copy)
    finish_lead(0)
    f_copies = []
    for d in range(pn.nlat):
        if d > 0:
            v_copies[d - 1].wait_recv()
        s = lax.rem(lat + pn.nlat - d, pn.nlat)
        copy = pltpu.make_async_remote_copy(
            src_ref=h_out.at[lon, s], dst_ref=h_out.at[lon, s],
            send_sem=f_s.at[d], recv_sem=f_r.at[d],
            device_id={"lon": other}, device_id_type=mesh_id,
        )
        copy.start()
        f_copies.append(copy)
    for copy in v_copies:
        copy.wait_send()
    for copy in f_copies:
        copy.wait()
    for copy in g_copies:
        copy.wait()


def finish_kernel(plan, modes, h_in, loc, lon_t, same, tile, spread, grad_out, mode_grad, buf, sem):
    pn = plan
    lon = lax.axis_index("lon")
    c = pn.c
    copies = []
    for p in range(pn.nlat):
        ch, cl = cut(modes[p, 0])
        sh, sl = cut(modes[p, 1])
        s4 = mm(sh, tile[...]) + mm(sl, tile[...])
        for k in range(pn.kp):
            chunk = p * pn.kp + k
            rows = slice(chunk * pn.lq, (chunk + 1) * pn.lq)
            four = s4[:, k * 128 : (k + 1) * 128]
            two = jnp.concatenate([four, four], axis=1)
            for j in range(pn.cc // 256):
                cols = slice(j * 256, (j + 1) * 256)
                big = mm(ch, spread[k, :, cols]) + mm(cl, spread[k, :, cols])
                buf[rows, cols] = big * two
            copy = pltpu.make_async_copy(buf.at[rows, :], mode_grad.at[rows, :], sem.at[chunk])
            copy.start()
            copies.append(copy)
    mask = same[:, 0:256]
    split = [[cut(h_in[a, b]) for b in range(pn.nlat)] for a in range(pn.nlon)]
    for step in range(pn.xl * c // 256):
        cols = slice(step * 256, (step + 1) * 256)
        total = loc[:, cols]
        for g in range(pn.nlon * pn.nlat):
            parts = []
            for h in range(2):
                rows = [lon_t[h, lon, k : k + 1, cols] * mask for k in range(g * pn.kp, (g + 1) * pn.kp)]
                parts.append(jnp.concatenate(rows, axis=0))
            hh, hl = split[g // pn.nlat][g % pn.nlat]
            total += mm(hh, parts[0]) + mm(hl, parts[0]) + mm(hh, parts[1])
        grad_out[:, cols] = total.astype(BF16)
    for copy in copies:
        copy.wait()


def fast_device(plan, activation, pre_activation, cotangent, mode_weight, local_weight):
    pn = plan
    merged = activation.shape[2]
    flat = [v.reshape(pn.zy, merged) for v in (activation, pre_activation, cotangent)]
    vm = pl.BlockSpec(memory_space=pltpu.VMEM)
    hbm = pl.BlockSpec(memory_space=pl.ANY)
    half = MX // pn.nlon * pn.c
    dma = pltpu.SemaphoreType.DMA
    modes, h, loc = pl.pallas_call(
        functools.partial(remote_kernel, pn),
        out_shape=(
            pltpu.VMEM((pn.nlat, 2, pn.lq, pn.kc), F32),
            pltpu.VMEM((pn.nlon, pn.nlat, pn.zy, pn.kc), F32),
            pltpu.VMEM((pn.zy, merged), F32),
        ),
        in_specs=[vm] * 3 + [hbm] + [vm] * 11,
        out_specs=(vm,) * 3,
        scratch_shapes=[
            pltpu.VMEM((2, MX * pn.c, merged), BF16),
            pltpu.VMEM((4 * pn.zy, merged), BF16),
            pltpu.VMEM((pn.nlon, half, 2 * pn.zy), F32),
            pltpu.VMEM((half, 2 * pn.zy), F32),
            pltpu.VMEM((pn.nlat - 1, pn.kc, 2 * pn.zy), F32),
            pltpu.VMEM((pn.nlat, pn.kc, 2 * pn.zy), F32),
            pltpu.VMEM((pn.nlead, 2, pn.zl * MY, pn.kc), F32),
            pltpu.VMEM((pn.kp * pn.lq, pn.cc), F32),
            pltpu.VMEM((pn.nlat, pn.zy, pn.kc), F32),
            dma, dma, dma,
            dma((pn.nlat - 1,)), dma((pn.nlat - 1,)),
            dma((2, pn.nlead - 1)), dma((2, pn.nlead - 1)),
            dma((2, pn.nlat - 1)), dma((2, pn.nlat - 1)),
            dma((pn.nlat - 1,)), dma((pn.nlat - 1,)),
            dma((pn.nlat,)), dma((pn.nlat,)),
        ],
        compiler_params=pltpu.CompilerParams(
            collective_id=0, has_side_effects=True, vmem_limit_bytes=56 * 2**20
        ),
        name="modes",
    )(
        *flat, mode_weight, local_weight, pn.lon_table, pn.same, pn.lat_table, pn.lead_table,
        pn.lead_back, pn.lat_back, pn.tile, pn.gather, pn.fan, pn.block,
    )
    grad, mode_grad = pl.pallas_call(
        functools.partial(finish_kernel, pn),
        out_shape=(
            jax.ShapeDtypeStruct((pn.zy, merged), BF16),
            jax.ShapeDtypeStruct((pn.nlat * pn.kp * pn.lq, pn.cc), F32),
        ),
        in_specs=[vm] * 7,
        out_specs=(vm, hbm),
        scratch_shapes=[
            pltpu.VMEM((pn.nlat * pn.kp * pn.lq, pn.cc), F32),
            dma((pn.nlat * pn.kp,)),
        ],
        compiler_params=pltpu.CompilerParams(vmem_limit_bytes=40 * 2**20),
        name="finish",
    )(modes, h, loc, pn.lon_table, pn.same, pn.tile, pn.spread)
    return grad.reshape(activation.shape), mode_grad


def solution(mesh):
    in_specs = (
        P("lead", "lat", "lon"),
        P("lead", "lat", "lon"),
        P("lead", "lat", "lon"),
        P("lon", None),
        P(),
    )
    out_specs = (P("lead", "lat", "lon"), P("lon", None))

    def whole(*args):
        shape = args[0].shape
        channels = args[4].shape[0]
        body = on_device
        if (
            mesh.shape["lon"] == 2
            and MX % (mesh.shape["lon"] * mesh.shape["lat"]) == 0
            and MX * MY * MZ == args[3].shape[0]
            and shape[2] // mesh.shape["lon"] % 256 == 0
            and 128 % channels == 0
        ):
            body = functools.partial(fast_device, Plan(mesh, shape, channels))
        return jax.shard_map(
            body, mesh=mesh, in_specs=in_specs, out_specs=out_specs, check_vma=False
        )(*args)

    return whole
```

```python
import functools
import math

import jax
import jax.numpy as jnp
import ml_dtypes
import numpy as np
from jax import lax
from jax.experimental import pallas as pl
from jax.experimental.pallas import tpu as pltpu
from jax.sharding import PartitionSpec as P

MX = 24
MY = 24
MZ = 8
MODES = 4608


def make_basis(length, modes, start, count, stride):
    half = modes // 2
    order = jnp.arange(modes, dtype=jnp.int32)
    freq = jnp.where(order < half, order, order - half + 1)
    cells = start + stride * jnp.arange(count, dtype=jnp.int32)
    turns = freq[:, None] * cells[None, :] % length
    angle = 2.0 * math.pi / length * turns.astype(jnp.float32)
    waves = jnp.where(order[:, None] < half, jnp.cos(angle), jnp.sin(angle))
    weights = jnp.where(
        order == 0, jnp.float32(math.sqrt(1.0 / length)), jnp.float32(math.sqrt(2.0 / length))
    )
    return waves * weights[:, None]


def gelu_slope(value):
    normal_cdf = 0.5 * (1.0 + jax.scipy.special.erf(value / math.sqrt(2.0)))
    density = jnp.exp(-0.5 * value * value) / math.sqrt(2.0 * math.pi)
    return normal_cdf + value * density


def back_cells(coeffs, lon_basis, lat_basis, lead_basis):
    highest = lax.Precision.HIGHEST
    blocks = coeffs.reshape(
        lon_basis.shape[0], lat_basis.shape[0], lead_basis.shape[0], coeffs.shape[-1]
    )
    step = jnp.einsum("klqc,qz->zklc", blocks, lead_basis, precision=highest)
    step = jnp.einsum("zklc,ly->zykc", step, lat_basis, precision=highest)
    return jnp.einsum("zykc,kx->zyxc", step, lon_basis, precision=highest)


def on_device(activation, pre_activation, cotangent, mode_weight, local_weight):
    highest = lax.Precision.HIGHEST
    channels = local_weight.shape[0]
    lead_cells, lat_cells, merged = activation.shape
    lon_cells = merged // channels
    lon_count = lax.axis_size("lon")
    lon_total = lon_cells * lon_count
    lat_total = lat_cells * lax.axis_size("lat")
    lead_total = lead_cells * lax.axis_size("lead")
    lon_basis = make_basis(lon_total, MX, lax.axis_index("lon"), lon_cells, lon_count)
    lat_basis = make_basis(lat_total, MY, lax.axis_index("lat") * lat_cells, lat_cells, 1)
    lead_basis = make_basis(lead_total, MZ, lax.axis_index("lead") * lead_cells, lead_cells, 1)
    shape4 = (lead_cells, lat_cells, lon_cells, channels)
    grad_pre = cotangent.astype(jnp.float32).reshape(shape4) * gelu_slope(
        pre_activation.astype(jnp.float32).reshape(shape4)
    )
    stacked = jnp.concatenate([activation.astype(jnp.float32).reshape(shape4), grad_pre], axis=3)
    doubled = 2 * channels
    along_lon = jnp.einsum("zyxc,kx->zykc", stacked, lon_basis, precision=highest)
    along_lat = jnp.einsum("zykc,ly->zklc", along_lon, lat_basis, precision=highest)
    partial_sum = jnp.einsum("zklc,qz->klqc", along_lat, lead_basis, precision=highest).reshape(
        -1, doubled
    )
    summed = lax.psum(partial_sum, ("lat", "lead"))
    owned = lax.psum_scatter(summed, "lon", scatter_dimension=0, tiled=True)
    gain = math.sqrt(lon_total * lat_total * lead_total / MODES)
    coef = owned[:, :channels]
    spectral = gain * owned[:, channels:]
    owned_count = owned.shape[0]
    mode_grad = (coef[:, :, None] * spectral[:, None, :]).reshape(owned_count, channels * channels)
    mixing = mode_weight.reshape(owned_count, channels, channels)
    owned_adjoint = jnp.sum(mixing * spectral[:, None, :], axis=2)
    every_mode = lax.all_gather(owned_adjoint, "lon", axis=0, tiled=True)
    spread = back_cells(every_mode, lon_basis, lat_basis, lead_basis)
    local = jnp.einsum("zyxo,io->zyxi", grad_pre, local_weight, precision=highest)
    input_grad = (spread + local).reshape(lead_cells, lat_cells, merged)
    return (input_grad.astype(jnp.bfloat16), mode_grad)


F32 = jnp.float32
BF16 = jnp.bfloat16


def host_basis(length, modes):
    half = modes // 2
    order = np.arange(modes)
    freq = np.where(order < half, order, order - half + 1)
    turns = (freq[:, None] * np.arange(length)[None, :]) % length
    angle = 2.0 * np.pi / length * turns
    waves = np.where(order[:, None] < half, np.cos(angle), np.sin(angle))
    weights = np.where(order == 0, np.sqrt(1.0 / length), np.sqrt(2.0 / length))
    return waves * weights[:, None]


def halves(table):
    table = np.asarray(table, np.float32)
    high = table.astype(ml_dtypes.bfloat16)
    low = (table - high.astype(np.float32)).astype(ml_dtypes.bfloat16)
    return np.stack([high, low])


def cut(value):
    high = value.astype(BF16)
    return high, (value - high.astype(F32)).astype(BF16)


NN = (((1,), (0,)), ((), ()))
NT = (((1,), (1,)), ((), ()))


def mm(a, b, dims=NN):
    return lax.dot_general(a, b, dims, preferred_element_type=F32)


def mm3(table, b, dims=NN):
    bh, bl = cut(b)
    return mm(table[0], bh, dims) + mm(table[0], bl, dims) + mm(table[1], bh, dims)


def placed(shape, axis, channels, base):
    wide = lax.broadcasted_iota(jnp.int32, shape, axis) // channels
    narrow = lax.broadcasted_iota(jnp.int32, shape, 1 - axis) - base
    return jnp.where(wide == narrow, 1.0, 0.0).astype(BF16)


def fold(value):
    r, lanes = value.shape[0] // 4, value.shape[1] // 3
    last = jnp.concatenate([value[3 * r :, g * lanes : (g + 1) * lanes] for g in range(3)], axis=0)
    return jnp.concatenate([value[: 3 * r], last], axis=1)


def unfold(value):
    r, lanes = value.shape[0] // 3, value.shape[1] // 4
    last = jnp.concatenate([value[g * r : (g + 1) * r, 3 * lanes :] for g in range(3)], axis=1)
    return jnp.concatenate([value[:, : 3 * lanes], last], axis=0)


class Plan:
    def __init__(self, mesh, arg_shape, channels):
        self.nlon, self.nlat, self.nlead = (mesh.shape[n] for n in ("lon", "lat", "lead"))
        nz, ny, merged = arg_shape
        self.c = channels
        self.zl, self.yl = nz // self.nlead, ny // self.nlat
        self.nx = merged // channels
        self.xl = self.nx // self.nlon
        self.kp = MX // (self.nlon * self.nlat)
        self.kc = self.kp * channels
        self.lq = MY * MZ
        self.zy = self.zl * self.yl
        self.gain = math.sqrt(self.nx * ny * nz / MODES)
        eye_z, eye_l = np.eye(self.zl), np.eye(MY)
        bx, by, bz = host_basis(self.nx, MX), host_basis(ny, MY), host_basis(nz, MZ)
        c = channels
        lon_rows = np.stack(
            [np.repeat(bx[:, d :: self.nlon], c, axis=1) for d in range(self.nlon)]
        )
        self.lon_table = halves(lon_rows)
        self.same = np.tile(np.eye(c), (1, self.xl)).astype(ml_dtypes.bfloat16)
        by_p = by.reshape(MY, self.nlat, self.yl)
        bz_s = bz.reshape(MZ, self.nlead, self.zl)
        eye_fz = np.eye(2 * self.zl)
        self.lat_table = halves(
            np.stack([np.kron(eye_fz, by_p[:, p]) for p in range(self.nlat)])
        )
        lead = np.einsum("qsz,lm->slqzm", bz_s, eye_l)
        self.lead_table = halves(lead.reshape(self.nlead, self.lq, self.zl * MY))
        self.lead_back = halves(
            lead.transpose(0, 3, 4, 1, 2).reshape(self.nlead, self.zl * MY, self.lq)
        )
        back = np.einsum("lpy,zw->pzywl", by_p, eye_z)
        self.lat_back = halves(back.reshape(self.nlat * self.zy, self.zl * MY))
        cc = c * c
        groups = 128 // c
        self.tile = np.concatenate(
            [np.kron(np.eye(groups)[:, [k]], np.tile(np.eye(c), (1, groups))) for k in range(groups)],
            axis=1,
        ).astype(ml_dtypes.bfloat16)
        wide = 256 // c
        self.fan = np.tile(np.eye(c), (1, wide)).astype(np.float32)
        self.block = np.kron(np.eye(wide), np.ones((c, c))).astype(np.float32)
        self.cc = cc


def remote_kernel(
    plan, act, pre, cot, weight, lw, lon_t, same, lat_t, lead_t, lead_b, lat_b, tile, fan, block,
    modes_out, h_out, loc_out,
    kx, xs, sbuf, lonbuf, latsend, latrecv, leadbuf, wbuf, vbuf,
    wsem, lon_s, lon_r, lat_s, lat_r, lead_s, lead_r, g_s, g_r, v_s, v_r, f_s, f_r,
):
    pn = plan
    lon, lat, lead = (lax.axis_index(n) for n in ("lon", "lat", "lead"))
    mesh_id = pl.DeviceIdType.MESH
    other = 1 - lon
    wcopy = pltpu.make_async_copy(
        weight.at[pl.ds(pl.multiple_of(lat * (pn.kp * pn.lq), 8), pn.kp * pn.lq), :], wbuf, wsem
    )
    wcopy.start()
    barrier = pltpu.get_barrier_semaphore()
    pl.semaphore_signal(barrier, inc=1, device_id={"lon": other}, device_id_type=mesh_id)
    for d in range(1, pn.nlat):
        pl.semaphore_signal(
            barrier, inc=1, device_id={"lat": lax.rem(lat + d, pn.nlat)}, device_id_type=mesh_id
        )
    for d in range(1, pn.nlead):
        pl.semaphore_signal(
            barrier, inc=1, device_id={"lead": lax.rem(lead + d, pn.nlead)}, device_id_type=mesh_id
        )
    c = pn.c
    zy = pn.zy
    mask = same[...]
    for k in range(MX):
        for h in range(2):
            kx[h, k * c : (k + 1) * c, :] = lon_t[h, lon, k : k + 1, :] * mask

    v = pre[...].astype(F32)
    cdf = 0.5 * (1.0 + lax.erf(v * (1.0 / math.sqrt(2.0))))
    density = jnp.exp(-0.5 * v * v) * (1.0 / math.sqrt(2.0 * math.pi))
    grad = cot[...].astype(F32) * (cdf + v * density)
    gh, gl = cut(grad)
    xs[0:zy, :] = act[...]
    xs[zy : 2 * zy, :] = gh
    xs[2 * zy : 3 * zy, :] = jnp.zeros_like(gh)
    xs[3 * zy : 4 * zy, :] = gl
    half = MX // pn.nlon * c
    for turn in range(2):
        who = other if turn == 0 else lon
        rows = pl.ds(pl.multiple_of(who * half, half), half)
        p = mm(kx[0, rows, :], xs[...], NT)
        q = mm(kx[1, rows, :], xs[0 : 2 * zy, :], NT)
        sbuf[who] = p[:, 0 : 2 * zy] + p[:, 2 * zy :] + q
        if turn == 0:
            pl.semaphore_wait(barrier, 1 + (pn.nlat - 1) + (pn.nlead - 1))
            lon_copy = pltpu.make_async_remote_copy(
                src_ref=sbuf.at[other], dst_ref=lonbuf, send_sem=lon_s, recv_sem=lon_r,
                device_id={"lon": other}, device_id_type=mesh_id,
            )
            lon_copy.start()
    lon_copy.wait()
    lat_copies = []
    for d in list(range(1, pn.nlat)) + [0]:
        p = lax.rem(lat + d, pn.nlat)
        rows = pl.ds(pl.multiple_of(p * pn.kc, pn.kc), pn.kc)
        value = sbuf[lon, rows, :] + lonbuf[rows, :]
        if d == 0:
            latrecv[lat] = value
        else:
            latsend[d - 1] = value
            copy = pltpu.make_async_remote_copy(
                src_ref=latsend.at[d - 1], dst_ref=latrecv.at[lat],
                send_sem=lat_s.at[d - 1], recv_sem=lat_r.at[d - 1],
                device_id={"lat": p}, device_id_type=mesh_id,
            )
            copy.start()
            lat_copies.append(copy)
    highest = lax.Precision.HIGHEST
    left = lax.dot_general(fan[...], lw[...], (((0,), (1,)), ((), ())), precision=highest, preferred_element_type=F32)
    both = jnp.dot(left, fan[...], precision=highest, preferred_element_type=F32) * block[...]
    bh, bl = cut(both)
    for t in range(pn.xl * c // 256):
        cols = slice(t * 256, (t + 1) * 256)
        hi, lo = xs[zy : 2 * zy, cols], xs[3 * zy : 4 * zy, cols]
        loc_out[:, cols] = mm(hi, bh) + mm(lo, bh) + mm(hi, bl)
    for copy in lat_copies:
        copy.wait()
    total = None
    for p in range(pn.nlat):
        term = mm3((lat_t[0, p], lat_t[1, p]), latrecv[p], NT)
        total = term if total is None else total + term
    zm = pn.zl * MY
    lead_copies = {}
    for f in (1, 0):
        leadbuf[lead, f] = fold(total[f * zm : (f + 1) * zm, :])
        for d in range(1, pn.nlead):
            copy = pltpu.make_async_remote_copy(
                src_ref=leadbuf.at[lead, f], dst_ref=leadbuf.at[lead, f],
                send_sem=lead_s.at[f, d - 1], recv_sem=lead_r.at[f, d - 1],
                device_id={"lead": lax.rem(lead + d, pn.nlead)}, device_id_type=mesh_id,
            )
            copy.start()
            lead_copies[f, d] = copy
    g_copies = []

    def finish_lead(f):
        for d in range(1, pn.nlead):
            lead_copies[f, d].wait()
        total = None
        for s in range(pn.nlead):
            term = mm3((lead_t[0, s], lead_t[1, s]), unfold(leadbuf[s, f]))
            total = term if total is None else total + term
        if f == 1:
            total = total * pn.gain
        modes_out[lat, f] = fold(total)
        for d in range(1, pn.nlat):
            copy = pltpu.make_async_remote_copy(
                src_ref=modes_out.at[lat, f], dst_ref=modes_out.at[lat, f],
                send_sem=g_s.at[f, d - 1], recv_sem=g_r.at[f, d - 1],
                device_id={"lat": lax.rem(lat + d, pn.nlat)}, device_id_type=mesh_id,
            )
            copy.start()
            g_copies.append(copy)
        return total

    spectral = finish_lead(1)
    wcopy.wait()
    sh, sl = cut(spectral)
    pick = tile[0 : pn.kc, 0 : pn.kp * 128]
    wide = mm(sh, pick) + mm(sl, pick)
    adjoint = None
    for k in range(pn.kp):
        four = wide[:, k * 128 : (k + 1) * 128]
        prod = wbuf[k * pn.lq : (k + 1) * pn.lq, :] * jnp.concatenate([four] * (pn.cc // 128), axis=1)
        ph, plow = cut(prod)
        pick = placed((pn.cc, pn.kc), 0, c, k * c)
        term = mm(ph, pick) + mm(plow, pick)
        adjoint = term if adjoint is None else adjoint + term
    mine = mm3((lead_b[0, lead], lead_b[1, lead]), adjoint)
    cells = mm3((lat_b[0], lat_b[1]), mine)
    for p in range(pn.nlat):
        vbuf[p] = fold(cells[p * zy : (p + 1) * zy, :])
    h_out[lon, lat] = vbuf[lat]
    v_copies = []
    for d in range(1, pn.nlat):
        p = lax.rem(lat + d, pn.nlat)
        copy = pltpu.make_async_remote_copy(
            src_ref=vbuf.at[p], dst_ref=h_out.at[lon, lat],
            send_sem=v_s.at[d - 1], recv_sem=v_r.at[d - 1],
            device_id={"lat": p}, device_id_type=mesh_id,
        )
        copy.start()
        v_copies.append(copy)
    finish_lead(0)
    f_copies = []
    for d in range(pn.nlat):
        if d > 0:
            v_copies[d - 1].wait_recv()
        s = lax.rem(lat + pn.nlat - d, pn.nlat)
        copy = pltpu.make_async_remote_copy(
            src_ref=h_out.at[lon, s], dst_ref=h_out.at[lon, s],
            send_sem=f_s.at[d], recv_sem=f_r.at[d],
            device_id={"lon": other}, device_id_type=mesh_id,
        )
        copy.start()
        f_copies.append(copy)
    for copy in v_copies:
        copy.wait_send()
    for copy in f_copies:
        copy.wait()
    for copy in g_copies:
        copy.wait()


def finish_kernel(plan, modes, h_in, loc, lon_t, same, tile, grad_out, mode_grad, buf, sem):
    pn = plan
    lon = lax.axis_index("lon")
    c = pn.c
    copies = []
    spread = [placed((128, pn.cc), 1, c, k * c) for k in range(pn.kp + 1)]
    quarter = pn.lq // 4
    for p in range(pn.nlat):
        ch, cl = cut(modes[p, 0])
        sh, sl = cut(modes[p, 1])
        s4 = mm(sh, tile[...]) + mm(sl, tile[...])
        for k in range(pn.kp):
            chunk = p * pn.kp + k
            part = slice(k * quarter, (k + 1) * quarter)
            whole = (slice(0, 3 * quarter), k, chunk * pn.lq)
            for source, which, first in (whole, (part, pn.kp, chunk * pn.lq + 3 * quarter)):
                four = s4[source, which * 128 : (which + 1) * 128]
                two = jnp.concatenate([four, four], axis=1)
                for j in range(pn.cc // 256):
                    cols = slice(j * 256, (j + 1) * 256)
                    big = mm(ch[source], spread[which][:, cols]) + mm(cl[source], spread[which][:, cols])
                    buf[first : first + four.shape[0], cols] = big * two
            rows = slice(chunk * pn.lq, (chunk + 1) * pn.lq)
            copy = pltpu.make_async_copy(buf.at[rows, :], mode_grad.at[rows, :], sem.at[chunk])
            copy.start()
            copies.append(copy)
    mask = same[:, 0:256]
    split = [[cut(unfold(h_in[a, b])) for b in range(pn.nlat)] for a in range(pn.nlon)]
    for step in range(pn.xl * c // 256):
        cols = slice(step * 256, (step + 1) * 256)
        total = loc[:, cols]
        for g in range(pn.nlon * pn.nlat):
            parts = []
            for h in range(2):
                rows = [lon_t[h, lon, k : k + 1, cols] * mask for k in range(g * pn.kp, (g + 1) * pn.kp)]
                parts.append(jnp.concatenate(rows, axis=0))
            hh, hl = split[g // pn.nlat][g % pn.nlat]
            total += mm(hh, parts[0]) + mm(hl, parts[0]) + mm(hh, parts[1])
        grad_out[:, cols] = total.astype(BF16)
    for copy in copies:
        copy.wait()


def fast_device(plan, activation, pre_activation, cotangent, mode_weight, local_weight):
    pn = plan
    merged = activation.shape[2]
    flat = [v.reshape(pn.zy, merged) for v in (activation, pre_activation, cotangent)]
    vm = pl.BlockSpec(memory_space=pltpu.VMEM)
    hbm = pl.BlockSpec(memory_space=pl.ANY)
    half = MX // pn.nlon * pn.c
    dma = pltpu.SemaphoreType.DMA
    modes, h, loc = pl.pallas_call(
        functools.partial(remote_kernel, pn),
        out_shape=(
            pltpu.VMEM((pn.nlat, 2, pn.lq // 4 * 3, 128), F32),
            pltpu.VMEM((pn.nlon, pn.nlat, pn.zy // 4 * 3, 128), F32),
            pltpu.VMEM((pn.zy, merged), F32),
        ),
        in_specs=[vm] * 3 + [hbm] + [vm] * 10,
        out_specs=(vm,) * 3,
        scratch_shapes=[
            pltpu.VMEM((2, MX * pn.c, merged), BF16),
            pltpu.VMEM((4 * pn.zy, merged), BF16),
            pltpu.VMEM((pn.nlon, half, 2 * pn.zy), F32),
            pltpu.VMEM((half, 2 * pn.zy), F32),
            pltpu.VMEM((pn.nlat - 1, pn.kc, 2 * pn.zy), F32),
            pltpu.VMEM((pn.nlat, pn.kc, 2 * pn.zy), F32),
            pltpu.VMEM((pn.nlead, 2, pn.zl * MY // 4 * 3, 128), F32),
            pltpu.VMEM((pn.kp * pn.lq, pn.cc), F32),
            pltpu.VMEM((pn.nlat, pn.zy // 4 * 3, 128), F32),
            dma, dma, dma,
            dma((pn.nlat - 1,)), dma((pn.nlat - 1,)),
            dma((2, pn.nlead - 1)), dma((2, pn.nlead - 1)),
            dma((2, pn.nlat - 1)), dma((2, pn.nlat - 1)),
            dma((pn.nlat - 1,)), dma((pn.nlat - 1,)),
            dma((pn.nlat,)), dma((pn.nlat,)),
        ],
        compiler_params=pltpu.CompilerParams(
            collective_id=0, has_side_effects=True, vmem_limit_bytes=56 * 2**20
        ),
        name="modes",
    )(
        *flat, mode_weight, local_weight, pn.lon_table, pn.same, pn.lat_table, pn.lead_table,
        pn.lead_back, pn.lat_back, pn.tile, pn.fan, pn.block,
    )
    grad, mode_grad = pl.pallas_call(
        functools.partial(finish_kernel, pn),
        out_shape=(
            jax.ShapeDtypeStruct((pn.zy, merged), BF16),
            jax.ShapeDtypeStruct((pn.nlat * pn.kp * pn.lq, pn.cc), F32),
        ),
        in_specs=[vm] * 6,
        out_specs=(vm, hbm),
        scratch_shapes=[
            pltpu.VMEM((pn.nlat * pn.kp * pn.lq, pn.cc), F32),
            dma((pn.nlat * pn.kp,)),
        ],
        compiler_params=pltpu.CompilerParams(vmem_limit_bytes=40 * 2**20),
        name="finish",
    )(modes, h, loc, pn.lon_table, pn.same, pn.tile)
    return grad.reshape(activation.shape), mode_grad


def solution(mesh):
    in_specs = (
        P("lead", "lat", "lon"),
        P("lead", "lat", "lon"),
        P("lead", "lat", "lon"),
        P("lon", None),
        P(),
    )
    out_specs = (P("lead", "lat", "lon"), P("lon", None))

    def whole(*args):
        shape = args[0].shape
        channels = args[4].shape[0]
        body = on_device
        if (
            mesh.shape["lon"] == 2
            and MX % (mesh.shape["lon"] * mesh.shape["lat"]) == 0
            and MX * MY * MZ == args[3].shape[0]
            and shape[2] // mesh.shape["lon"] % 256 == 0
            and 4 * channels == 128
            and MX * channels == 96 * mesh.shape["lon"] * mesh.shape["lat"]
            and mesh.shape["lead"] * 4 == shape[0]
        ):
            body = functools.partial(fast_device, Plan(mesh, shape, channels))
        return jax.shard_map(
            body, mesh=mesh, in_specs=in_specs, out_specs=out_specs, check_vma=False
        )(*args)

    return whole
```
